256 devices in a mesh: section: 16 (over z, x_hi), head: 4 (over y), key: 4 (over x_lo, core).
Axes of the slice: x: 4 (x_hi: 2, x_lo: 2; x = x_hi * 2 + x_lo), y: 4, z: 8, core: 2. Of those that a mesh axis runs over, the one named last changes fastest.
Arguments:
- queries: bfloat16 [16, 256, 3072], P('section', None, 'head'), may hold values from -1024 to 1024
- attn_grad: bfloat16 [16, 256, 3072], P('section', None, 'head'), may hold values from -192 to 192
- query_weight: bfloat16 [16, 3072, 3072], P('section', None, 'head'), may hold values from -0.109375 to 0.109375
- key_codes: int32 [4096, 1024], P('key', 'head'), may hold values from -127 to 127
- key_exps: int32 [64, 8], P('key', 'head'), may hold values from -9 to -6
- value_codes: int32 [4096, 1024], P('key', 'head'), may hold values from -127 to 127
- value_exps: int32 [64, 8], P('key', 'head'), may hold values from -9 to -6
Outputs:
- input_grad: bfloat16 [16, 256, 3072], P('section', ('head', 'key'))
- key_grad: float32 [4096, 1024], P(('key', 'section'), 'head')
- value_grad: float32 [4096, 1024], P(('key', 'section'), 'head')
The draws below stay inside these ranges and needn't reach their ends.
All inputs are finite; a program needn't handle non-finite values.
Results may differ from the reference program's by a relative error of at most 0.017.
Values may be sent and summed in bfloat16 or wider, within the bound.
No kernel may reach another device: no remote copies, remote signals or barrier semaphores. Data moves between devices by JAX's collectives and lax.ppermute only.
A program may use at most 64 MiB of HBM per device.

```python
import math
import jax
import jax.numpy as jnp
from jax import lax

D = 3072
HQ = 24
KVH = 8
HD = 128
S = 4096
BLK = 64
ROWS = 256
LAYERS = 16
N_HEAD = 4


def key_code_table(key):
    return jax.random.randint(jax.random.fold_in(key, 101), (S, KVH * HD), -127, 128, dtype=jnp.int32)


def key_exponent_table(key):
    return jax.random.randint(jax.random.fold_in(key, 102), (S // BLK, KVH), -9, -5, dtype=jnp.int32)


def draw_key_codes(key, part):
    return key_code_table(key)


def draw_key_exps(key, part):
    return key_exponent_table(key)


def draw_queries(key, part):
    full_shape = (LAYERS, ROWS, HQ * HD)
    row_scale = jnp.exp(jax.random.uniform(jax.random.fold_in(key, 201), (LAYERS, ROWS, 1), minval=math.log(0.25), maxval=math.log(2.5)))
    base_draw = jax.random.normal(jax.random.fold_in(key, 202), full_shape, jnp.float32)
    drawn_draw = 0.3 * row_scale * base_draw
    return jnp.clip(drawn_draw, -1024.0, 1024.0).astype(jnp.bfloat16)


def with_ends(entries, rng, least, top_value):
    longest = entries.shape.index(max(entries.shape))
    spots = []
    for shift in (0, 1):
        where = [jax.random.randint(jax.random.fold_in(rng, axis), (), 0, length) for axis, length in enumerate(entries.shape)]
        where[longest] = (where[longest] + shift) % entries.shape[longest]
        spots.append(tuple(where))
    return entries.at[spots[0]].set(least).at[spots[1]].set(top_value)


def block_levels(stream_key, dims, shards, smallest, high):
    factor_of = 1.0
    for axis_at, blocks in shards:
        heights = jax.random.uniform(jax.random.fold_in(jax.random.fold_in(stream_key, 6), axis_at), (blocks,), jnp.float32, smallest / len(shards), high / len(shards))
        factor_of = factor_of * jnp.repeat(jnp.exp(heights), dims[axis_at] // blocks).reshape((-1,) + (1,) * (len(dims) - 1 - axis_at))
    return factor_of


def bell_draw(stream_key, dims, spread, bound, cuts=(), kind=jnp.bfloat16):
    values = jax.random.normal(stream_key, dims, jnp.float32) * spread
    if len(cuts) > 0:
        values = block_levels(stream_key, dims, cuts, -0.22, 0.18) * values
    return jnp.clip(values, min=-bound, max=bound).astype(kind)


def setup_inputs(seed: int = 0) -> dict:
    seeds = jax.random.split(jax.random.key(seed), 8)
    return {
        "queries": draw_queries(jax.random.fold_in(seeds[7], 71), 0),
        "attn_grad": bell_draw(seeds[1], (LAYERS, ROWS, HQ * HD), 32.0, 192.0, ((0, 16), (2, 4))),
        "query_weight": bell_draw(seeds[2], (LAYERS, D, HQ * HD), D ** -0.5, 0.109375, ((0, 16), (2, 4))),
        "key_codes": draw_key_codes(jax.random.fold_in(seeds[7], 71), 0),
        "key_exps": draw_key_exps(jax.random.fold_in(seeds[7], 71), 0),
        "value_codes": with_ends(jax.random.randint(seeds[5], (S, KVH * HD), -127, 128), jax.random.fold_in(seeds[5], 1), -127, 127).astype(jnp.int32),
        "value_exps": with_ends(jax.random.randint(seeds[6], (S // BLK, KVH), -9, -5), jax.random.fold_in(seeds[6], 1), -9, (-5) - 1).astype(jnp.int32),
    }


def dequantize(code_array, exponents):
    factor = jnp.exp2(exponents.astype(jnp.float32))
    factor = jnp.repeat(factor, BLK, axis=0)
    shaped = code_array.astype(jnp.float32).reshape(S, KVH, HD)
    return (shaped * factor[:, :, None]).astype(jnp.bfloat16)


def per_head(head_args):
    query_head, grad_head, key_head, value_head = head_args
    query_f = query_head.astype(jnp.float32)
    grad_f = grad_head.astype(jnp.float32)
    key_f = key_head.astype(jnp.float32)
    value_f = value_head.astype(jnp.float32)
    score_scale = HD ** -0.5
    scores = jnp.einsum('rgd,sd->grs', query_f, key_f) * score_scale
    row_max = jnp.max(scores, axis=-1, keepdims=True)
    shifted = jnp.exp(scores - row_max)
    probs = shifted / jnp.sum(shifted, axis=-1, keepdims=True)
    grad_probs = jnp.einsum('rgd,sd->grs', grad_f, value_f)
    row_delta = jnp.sum(probs * grad_probs, axis=-1, keepdims=True)
    grad_scores = probs * (grad_probs - row_delta)
    probs_low = lax.optimization_barrier(probs.astype(jnp.bfloat16)).astype(jnp.float32)
    grads_low = lax.optimization_barrier(grad_scores.astype(jnp.bfloat16)).astype(jnp.float32)
    key_part = jnp.einsum('grs,rgd->sd', grads_low, query_f) * score_scale
    value_part = jnp.einsum('grs,rgd->sd', probs_low, grad_f)
    query_part = jnp.einsum('grs,sd->rgd', grads_low, key_f) * score_scale
    return key_part, value_part, query_part


def reference(queries, attn_grad, query_weight, key_codes, key_exps, value_codes, value_exps):
    key_vals = dequantize(key_codes, key_exps).transpose(1, 0, 2)
    value_vals = dequantize(value_codes, value_exps).transpose(1, 0, 2)
    group_size = HQ // KVH
    head_cols = HQ // N_HEAD * HD

    def layer_step(carry_sums, inputs):
        key_sum, value_sum = carry_sums
        query_rows, grad_rows, weight = inputs
        query_heads = query_rows.reshape(ROWS, KVH, group_size, HD).transpose(1, 0, 2, 3)
        grad_heads = grad_rows.reshape(ROWS, KVH, group_size, HD).transpose(1, 0, 2, 3)
        key_part, value_part, query_part = lax.map(per_head, (query_heads, grad_heads, key_vals, value_vals))
        query_grad = query_part.transpose(1, 0, 2, 3).reshape(ROWS, HQ * HD).astype(jnp.bfloat16)
        query_groups = lax.optimization_barrier(query_grad).astype(jnp.float32).reshape(ROWS, N_HEAD, head_cols)
        weight_groups = weight.astype(jnp.float32).reshape(D, N_HEAD, head_cols)
        partial_value = jnp.einsum('rgc,dgc->grd', query_groups, weight_groups)
        partial_value = lax.optimization_barrier(partial_value.astype(jnp.bfloat16)).astype(jnp.float32)
        input_grad = jnp.sum(partial_value, axis=0).astype(jnp.bfloat16)
        return (key_sum + key_part, value_sum + value_part), input_grad

    zero_sums = jnp.zeros((KVH, S, HD), jnp.float32)
    final_sums, input_grad = lax.scan(layer_step, (zero_sums, zero_sums), (queries, attn_grad, query_weight))
    key_grad = final_sums[0].transpose(1, 0, 2).reshape(S, KVH * HD)
    value_grad = final_sums[1].transpose(1, 0, 2).reshape(S, KVH * HD)
    return input_grad, key_grad, value_grad
```

```python
import jax
import jax.numpy as jnp
from jax import lax
from jax.experimental import pallas as pl
from jax.experimental.pallas import tpu as pltpu
from jax.sharding import PartitionSpec as P

HQ = 24
KVH = 8
HD = 128
GROUP = HQ // KVH
ROWS = 256
BLK = 64
LOG2E = 1.4426950408889634
SCALE = HD ** -0.5
LEAST_EXP = -9

F32 = jnp.float32
BF16 = jnp.bfloat16

VMEM = pl.BlockSpec(memory_space=pltpu.VMEM)
SMEM = pl.BlockSpec(memory_space=pltpu.SMEM)


def dot(a, b, dims):
    return lax.dot_general(a, b, (dims, ((), ())), preferred_element_type=F32)


def local_kernel(exps_k, exps_v, q_ref, d_ref, kc_ref, vc_ref, e_ref, dp_ref, k_ref, kt_ref, stat_ref, v_ref):
    keys = kc_ref.shape[0]
    half = keys // 2
    for g in range(2):
        wide = slice(g * HD, (g + 1) * HD)
        for b in range(keys // BLK):
            at = slice(b * BLK, (b + 1) * BLK)
            for exps, codes, out in ((exps_k, kc_ref, k_ref), (exps_v, vc_ref, v_ref)):
                power = jnp.left_shift(1, exps[g, b] - LEAST_EXP).astype(F32) * (2.0 ** LEAST_EXP)
                out[at, wide] = (codes[at, wide].astype(F32) * power).astype(BF16)
        kt_ref[wide, :] = k_ref[:, wide].T
        for h in range(GROUP):
            head = g * GROUP + h
            cols = slice(head * HD, (head + 1) * HD)
            q = q_ref[:, cols]
            d = d_ref[:, cols]
            top = None
            for c in range(2):
                at = slice(c * half, (c + 1) * half)
                s = dot(k_ref[at, wide], q, ((1,), (1,)))
                dp_ref[head, at, :] = s
                part = jnp.max(s, axis=0, keepdims=True)
                top = part if top is None else jnp.maximum(top, part)
            total = jnp.zeros((1, ROWS), F32)
            inner = jnp.zeros((1, ROWS), F32)
            for c in range(2):
                at = slice(c * half, (c + 1) * half)
                e = jnp.exp2((dp_ref[head, at, :] - top) * (SCALE * LOG2E))
                e_ref[head, at, :] = e
                total += jnp.sum(e, axis=0, keepdims=True)
                dp = dot(v_ref[at, wide], d, ((1,), (1,)))
                dp_ref[head, at, :] = dp
                inner += jnp.sum(e * dp, axis=0, keepdims=True)
            stat_ref[head:head + 1, :] = top * (SCALE * LOG2E)
            stat_ref[8 + head:9 + head, :] = total
            stat_ref[16 + head:17 + head, :] = inner


def grad_kernel(*refs):
    stats, (e_ref, dp_ref, kt_ref, q_ref, d_ref, kv_ref, qg_ref) = refs[:4], refs[4:]
    top = stats[0][0:8, :]
    for s in stats[1:]:
        top = jnp.maximum(top, s[0:8, :])
    weights = [jnp.exp2(s[0:8, :] - top) for s in stats]
    total = sum(w * s[8:16, :] for w, s in zip(weights, stats))
    inner = sum(w * s[16:24, :] for w, s in zip(weights, stats))
    delta = inner / total
    mine = weights[0] / total
    for g in range(2):
        wide = slice(g * HD, (g + 1) * HD)
        key_sum = value_sum = None
        for h in range(GROUP):
            head = g * GROUP + h
            cols = slice(head * HD, (head + 1) * HD)
            p = e_ref[head] * mine[head:head + 1, :]
            ds = (p * (dp_ref[head] - delta[head:head + 1, :])).astype(BF16)
            kg = dot(ds, q_ref[:, cols], ((1,), (0,)))
            vg = dot(p.astype(BF16), d_ref[:, cols], ((1,), (0,)))
            key_sum = kg if h == 0 else key_sum + kg
            value_sum = vg if h == 0 else value_sum + vg
            qt = dot(kt_ref[wide, :], ds, ((1,), (0,)))
            qg = (qt.T * SCALE).astype(BF16)
            for a in range(4):
                for k in range(4):
                    qg_ref[k, a * 16:(a + 1) * 16, cols] = qg[(a * 4 + k) * 16:(a * 4 + k + 1) * 16, :]
        kv_ref[:, g * HD:(g + 1) * HD] = (key_sum * SCALE).astype(BF16)
        kv_ref[:, (2 + g) * HD:(3 + g) * HD] = value_sum.astype(BF16)


def project_kernel(a_ref, b_ref, c_ref, d_ref, w_ref, o_ref):
    total = sum(r[...].astype(F32) for r in (a_ref, b_ref, c_ref, d_ref)).astype(BF16)
    o_ref[...] = dot(total, w_ref[...], ((1,), (1,))).astype(BF16)


def finish_kernel(kv_ref, a_ref, b_ref, c_ref, d_ref, key_ref, value_ref, input_ref):
    total = kv_ref[0].astype(F32)
    for k in range(1, kv_ref.shape[0]):
        total += kv_ref[k].astype(F32)
    width = key_ref.shape[1]
    key_ref[...] = total[:, :width]
    value_ref[...] = total[:, width:]
    input_ref[...] = sum(r[...].astype(F32) for r in (a_ref, b_ref, c_ref, d_ref)).astype(BF16)


def shifted(x, axis, by):
    n = lax.axis_size(axis)
    return lax.ppermute(x, axis, [(i, (i + by) % n) for i in range(n)])


def spread(blocks, axis):
    n = lax.axis_size(axis)
    me = lax.axis_index(axis)
    pick = lambda by: lax.dynamic_index_in_dim(blocks, (me + by) % n, 0, keepdims=False)
    return [pick(0)] + [shifted(pick(by), axis, by) for by in range(1, n)]


def body(queries, attn_grad, query_weight, key_codes, key_exps, value_codes, value_exps):
    q, d, w = queries[0], attn_grad[0], query_weight[0]
    keys = key_codes.shape[0]
    heads = q.shape[1] // HD
    width = key_codes.shape[1]
    out = lambda shape, dtype: pltpu.VMEM(shape, dtype)
    e, dp, k, kt, stat = pl.pallas_call(
        local_kernel,
        in_specs=[SMEM, SMEM, VMEM, VMEM, VMEM, VMEM],
        out_specs=[VMEM] * 5,
        out_shape=[out((heads, keys, ROWS), F32),
                   out((heads, keys, ROWS), F32),
                   out((keys, width), BF16),
                   out((width, keys), BF16),
                   out((24, ROWS), F32)],
        scratch_shapes=[pltpu.VMEM((keys, width), BF16)],
        compiler_params=pltpu.CompilerParams(vmem_limit_bytes=24 << 20),
        name="local",
    )(key_exps.T, value_exps.T, q, d, key_codes, value_codes)
    stats = [stat] + [shifted(stat, "key", by) for by in range(1, 4)]
    kv, qg = pl.pallas_call(
        grad_kernel,
        in_specs=[VMEM] * 9,
        out_specs=[VMEM] * 2,
        out_shape=[jax.ShapeDtypeStruct((keys, 2 * width), BF16),
                   jax.ShapeDtypeStruct((4, ROWS // 4, heads * HD), BF16)],
        compiler_params=pltpu.CompilerParams(vmem_limit_bytes=24 << 20),
        name="grad",
    )(*stats, e, dp, kt, q, d)
    kv = lax.all_to_all(kv.reshape(16, keys // 16, 2 * width), "section", 0, 0, tiled=True)
    parts = spread(qg, "key")
    d_model = w.shape[0]
    tile = 512
    rows = ROWS // 4
    whole = pl.BlockSpec((rows, heads * HD), lambda i: (0, 0))
    proj = pl.pallas_call(
        project_kernel,
        grid=(d_model // tile,),
        in_specs=[whole] * 4 + [pl.BlockSpec((tile, heads * HD), lambda i: (i, 0))],
        out_specs=pl.BlockSpec((rows, tile), lambda i: (0, i)),
        out_shape=jax.ShapeDtypeStruct((rows, d_model), BF16),
        compiler_params=pltpu.CompilerParams(vmem_limit_bytes=16 << 20),
        name="project",
    )(*parts, w)
    parts = spread(proj.reshape(4, rows // 4, d_model), "head")
    key_grad, value_grad, input_grad = pl.pallas_call(
        finish_kernel,
        in_specs=[VMEM] * 5,
        out_specs=[VMEM] * 3,
        out_shape=[jax.ShapeDtypeStruct((keys // 16, width), F32),
                   jax.ShapeDtypeStruct((keys // 16, width), F32),
                   jax.ShapeDtypeStruct((rows // 4, d_model), BF16)],
        compiler_params=pltpu.CompilerParams(vmem_limit_bytes=16 << 20),
        name="finish",
    )(kv, *parts)
    return input_grad[None], key_grad, value_grad


def solution(mesh):
    return jax.shard_map(
        body,
        mesh=mesh,
        in_specs=(
            P("section", None, "head"),
            P("section", None, "head"),
            P("section", None, "head"),
            P("key", "head"),
            P("key", "head"),
            P("key", "head"),
            P("key", "head"),
        ),
        out_specs=(
            P("section", ("head", "key"), None),
            P(("key", "section"), "head"),
            P(("key", "section"), "head"),
        ),
        check_vma=False,
    )
```

```python
import jax
import jax.numpy as jnp
from jax import lax
from jax.experimental import pallas as pl
from jax.experimental.pallas import tpu as pltpu
from jax.sharding import PartitionSpec as P

HQ = 24
KVH = 8
HD = 128
GROUP = HQ // KVH
ROWS = 256
BLK = 64
LOG2E = 1.4426950408889634
SCALE = HD ** -0.5
LEAST_EXP = -9
SECTIONS = 16
DEPTH = 8
W_TILES = 6

F32 = jnp.float32
BF16 = jnp.bfloat16

VMEM = pl.BlockSpec(memory_space=pltpu.VMEM)
HBM = pl.BlockSpec(memory_space=pl.ANY)


def dot(a, b, dims):
    return lax.dot_general(a, b, (dims, ((), ())), preferred_element_type=F32)


def local_kernel(exps_k, exps_v, q_hbm, d_hbm, kc_hbm, vc_hbm,
                 e_ref, dp_ref, kt_ref, stat_ref, q_ref, d_ref,
                 kc_ref, vc_ref, k_ref, v_ref, ke_ref, ve_ref, sems):
    sources = (exps_k, exps_v, kc_hbm, q_hbm, vc_hbm, d_hbm)
    targets = (ke_ref, ve_ref, kc_ref, q_ref, vc_ref, d_ref)
    copies = [pltpu.make_async_copy(s, t, sems.at[n]) for n, (s, t) in enumerate(zip(sources, targets))]
    for c in copies:
        c.start()
    keys = kc_ref.shape[0]
    half = keys // 2

    def dequantize(exps, codes, out):
        for g in range(2):
            wide = slice(g * HD, (g + 1) * HD)
            for b in range(keys // BLK):
                at = slice(b * BLK, (b + 1) * BLK)
                power = jnp.left_shift(1, exps[g, b] - LEAST_EXP).astype(F32) * (2.0 ** LEAST_EXP)
                out[at, wide] = (codes[at, wide].astype(F32) * power).astype(BF16)

    copies[0].wait()
    copies[2].wait()
    dequantize(ke_ref, kc_ref, k_ref)
    copies[3].wait()
    for head in range(2 * GROUP):
        g = head // GROUP
        wide = slice(g * HD, (g + 1) * HD)
        cols = slice(head * HD, (head + 1) * HD)
        q = q_ref[:, cols]
        if head == 0:
            copies[1].wait()
            copies[4].wait()
            dequantize(ve_ref, vc_ref, v_ref)
            copies[5].wait()
        d = d_ref[:, cols]
        top = None
        for c in range(2):
            at = slice(c * half, (c + 1) * half)
            s = dot(k_ref[at, wide], q, ((1,), (1,)))
            dp_ref[head, at, :] = s
            part = jnp.max(s, axis=0, keepdims=True)
            top = part if top is None else jnp.maximum(top, part)
        total = jnp.zeros((1, ROWS), F32)
        inner = jnp.zeros((1, ROWS), F32)
        for c in range(2):
            at = slice(c * half, (c + 1) * half)
            e = jnp.exp2((dp_ref[head, at, :] - top) * (SCALE * LOG2E))
            e_ref[head, at, :] = e
            total += jnp.sum(e, axis=0, keepdims=True)
            dp = dot(v_ref[at, wide], d, ((1,), (1,)))
            dp_ref[head, at, :] = dp
            inner += jnp.sum(e * dp, axis=0, keepdims=True)
        stat_ref[head:head + 1, :] = top * (SCALE * LOG2E)
        stat_ref[8 + head:9 + head, :] = total
        stat_ref[16 + head:17 + head, :] = inner
    for g in range(2):
        wide = slice(g * HD, (g + 1) * HD)
        kt_ref[wide, :] = k_ref[:, wide].T


def cache_grad_kernel(*refs):
    stats, (e_ref, dp_ref, q_ref, d_ref, ds_ref, keep_ref, send_v, send_k, both) = refs[:4], refs[4:]
    top = stats[0][0:8, :]
    for s in stats[1:]:
        top = jnp.maximum(top, s[0:8, :])
    weights = [jnp.exp2(s[0:8, :] - top) for s in stats]
    total = sum(w * s[8:16, :] for w, s in zip(weights, stats))
    inner = sum(w * s[16:24, :] for w, s in zip(weights, stats))
    delta = inner / total
    mine = weights[0] / total
    slab = both.shape[2]
    for g in range(2):
        for h in range(GROUP):
            head = g * GROUP + h
            cols = slice(head * HD, (head + 1) * HD)
            p = e_ref[head] * mine[head:head + 1, :]
            ds = (p * (dp_ref[head] - delta[head:head + 1, :])).astype(BF16)
            ds_ref[head] = ds
            kg = dot(ds, q_ref[:, cols], ((1,), (0,)))
            vg = dot(p.astype(BF16), d_ref[:, cols], ((1,), (0,)))
            key_sum = kg if h == 0 else key_sum + kg
            value_sum = vg if h == 0 else value_sum + vg
        key_low = (key_sum * SCALE).astype(BF16)
        value_low = value_sum.astype(BF16)
        for z in range(DEPTH):
            at = slice(z * slab, (z + 1) * slab)
            both[z % 2, z // 2, :, g * HD:(g + 1) * HD] = key_low[at, :]
            both[z % 2, z // 2, :, (2 + g) * HD:(3 + g) * HD] = value_low[at, :]
    side = lax.rem(lax.axis_index("section") // 2, 2)
    keep_ref[...] = both[side]
    send_k[...] = both[1 - side, :, :, :2 * HD]
    send_v[...] = both[1 - side, :, :, 2 * HD:]


def query_grad_kernel(ds_ref, kt_ref, o0, o1, o2, o3, all_ref):
    for head in range(2 * GROUP):
        g = head // GROUP
        cols = slice(head * HD, (head + 1) * HD)
        qt = dot(kt_ref[g * HD:(g + 1) * HD, :], ds_ref[head], ((1,), (0,)))
        qg = (qt.T * SCALE).astype(BF16)
        for a in range(4):
            for k in range(4):
                all_ref[k, a * 16:(a + 1) * 16, cols] = qg[(a * 4 + k) * 16:(a * 4 + k + 1) * 16, :]
    me = lax.axis_index("key")
    for by, o in enumerate((o0, o1, o2, o3)):
        o[...] = all_ref[jnp.bitwise_xor(me, by)]


def pair_kernel(keep_ref, key_ref, value_ref, out_ref):
    w = key_ref.shape[-1]
    out_ref[:, :, :w] = (keep_ref[:, :, :w].astype(F32) + key_ref[...].astype(F32)).astype(BF16)
    out_ref[:, :, w:] = (keep_ref[:, :, w:].astype(F32) + value_ref[...].astype(F32)).astype(BF16)


def project_kernel(a_ref, b_ref, c_ref, d_ref, w_hbm, o0, o1, o2, o3, all_ref, w_ref, sems):
    tile = w_ref.shape[0] // W_TILES
    tiles = [slice(n * tile, (n + 1) * tile) for n in range(W_TILES)]
    copies = [pltpu.make_async_copy(w_hbm.at[at, :], w_ref.at[at, :], sems.at[n]) for n, at in enumerate(tiles)]
    for c in copies:
        c.start()
    total = sum(r[...].astype(F32) for r in (a_ref, b_ref, c_ref, d_ref)).astype(BF16)
    for at, c in zip(tiles, copies):
        c.wait()
        part = dot(total, w_ref[at, :], ((1,), (1,))).astype(BF16)
        for k in range(4):
            all_ref[k, :, at] = part[k * 16:(k + 1) * 16, :]
    me = lax.axis_index("head")
    for by, o in enumerate((o0, o1, o2, o3)):
        o[...] = all_ref[lax.rem(me + by, 4)]


def finish_kernel(kv_ref, a_ref, b_ref, c_ref, d_ref, key_ref, value_ref, input_ref):
    total = kv_ref[0].astype(F32)
    for k in range(1, kv_ref.shape[0]):
        total += kv_ref[k].astype(F32)
    width = key_ref.shape[1]
    key_ref[...] = total[:, :width]
    value_ref[...] = total[:, width:]
    input_ref[...] = sum(r[...].astype(F32) for r in (a_ref, b_ref, c_ref, d_ref)).astype(BF16)


def moved(x, axis, to):
    return lax.ppermute(x, axis, [(i, to(i)) for i in range(lax.axis_size(axis))])


def deeper(section, by):
    return (section // 2 + by) % DEPTH * 2 + section % 2


def call(kernel, name, outs, ins, scratch=(), limit=16, specs=None):
    return pl.pallas_call(
        kernel,
        in_specs=specs or [VMEM] * len(ins),
        out_specs=[VMEM] * len(outs),
        out_shape=outs,
        scratch_shapes=scratch,
        compiler_params=pltpu.CompilerParams(vmem_limit_bytes=limit << 20),
        name=name,
    )(*ins)


def body(queries, attn_grad, query_weight, key_codes, key_exps, value_codes, value_exps):
    q, d, w = queries[0], attn_grad[0], query_weight[0]
    keys, width = key_codes.shape
    heads = q.shape[1] // HD
    d_model = w.shape[0]
    on = pltpu.VMEM
    e, dp, kt, stat, q, d = call(
        local_kernel, "local",
        [on((heads, keys, ROWS), F32), on((heads, keys, ROWS), F32), on((width, keys), BF16),
         on((24, ROWS), F32), on(q.shape, BF16), on(d.shape, BF16)],
        [pltpu.with_memory_space_constraint(x, pltpu.HBM)
         for x in (key_exps.T, value_exps.T, q, d, key_codes, value_codes)],
        scratch=[on(key_codes.shape, jnp.int32), on(key_codes.shape, jnp.int32),
                 on(key_codes.shape, BF16), on(key_codes.shape, BF16),
                 pltpu.SMEM(key_exps.shape[::-1], jnp.int32), pltpu.SMEM(key_exps.shape[::-1], jnp.int32),
                 pltpu.SemaphoreType.DMA((6,))],
        limit=16, specs=[HBM] * 6,
    )
    stats = [stat] + [moved(stat, "key", lambda i: i ^ by) for by in (1, 2, 3)]
    slab = keys // DEPTH
    half = (DEPTH // 2, slab, width)
    ds, keep, send_v, send_k = call(
        cache_grad_kernel, "cache_grad",
        [on((heads, keys, ROWS), BF16), on((*half[:2], 2 * width), BF16), on(half, BF16), on(half, BF16)],
        (*stats, e, dp, q, d),
        scratch=[on((2, *half[:2], 2 * width), BF16)],
    )
    got_v = moved(send_v, "section", lambda i: deeper(i, 1 - 2 * (i // 2 % 2)))
    got_k = moved(send_k, "section", lambda i: deeper(i, 2 * (i // 2 % 2) - 1))
    rows = ROWS // 4
    parts = call(
        query_grad_kernel, "query_grad",
        [on((rows, heads * HD), BF16)] * 4, (ds, kt),
        scratch=[on((4, rows, heads * HD), BF16)],
    )
    parts = [parts[0]] + [moved(parts[by], "key", lambda i: i ^ by) for by in (1, 2, 3)]
    keep, parts = lax.optimization_barrier((keep, parts))
    (kv,) = call(pair_kernel, "pair", [jax.ShapeDtypeStruct((*half[:2], 2 * width), BF16)], (keep, got_k, got_v))
    _, parts = lax.optimization_barrier((kv, parts))
    groups = [[(2 * a + p) * 2 + xh for a in range(DEPTH // 2) for xh in range(2)] for p in range(2)]
    kv = lax.all_to_all(
        kv.reshape(DEPTH, slab // 2, 2 * width), "section", 0, 0, axis_index_groups=groups, tiled=True
    )
    parts = call(
        project_kernel, "project",
        [on((rows // 4, d_model), BF16)] * 4,
        (*parts, pltpu.with_memory_space_constraint(w, pltpu.HBM)),
        scratch=[on((4, rows // 4, d_model), BF16), on(w.shape, BF16), pltpu.SemaphoreType.DMA((W_TILES,))],
        specs=[VMEM] * 4 + [HBM],
    )
    parts = [parts[0]] + [moved(parts[by], "head", lambda i: (i + by) % 4) for by in (1, 2, 3)]
    key_grad, value_grad, input_grad = call(
        finish_kernel, "finish",
        [jax.ShapeDtypeStruct((slab // 2, width), F32), jax.ShapeDtypeStruct((slab // 2, width), F32),
         jax.ShapeDtypeStruct((rows // 4, d_model), BF16)],
        (kv, *parts),
    )
    return input_grad[None], key_grad, value_grad


def solution(mesh):
    return jax.shard_map(
        body,
        mesh=mesh,
        in_specs=(
            P("section", None, "head"),
            P("section", None, "head"),
            P("section", None, "head"),
            P("key", "head"),
            P("key", "head"),
            P("key", "head"),
            P("key", "head"),
        ),
        out_specs=(
            P("section", ("head", "key"), None),
            P(("key", "section"), "head"),
            P(("key", "section"), "head"),
        ),
        check_vma=False,
    )
```

```python
import jax
import jax.numpy as jnp
from jax import lax
from jax.experimental import pallas as pl
from jax.experimental.pallas import tpu as pltpu
from jax.sharding import PartitionSpec as P


HQ = 24
KVH = 8
HD = 128
GROUP = HQ // KVH
ROWS = 256
BLK = 64
LOG2E = 1.4426950408889634
SCALE = HD ** -0.5
LEAST_EXP = -9
DEPTH = 8
W_TILES = 6

F32 = jnp.float32
BF16 = jnp.bfloat16

VMEM = pl.BlockSpec(memory_space=pltpu.VMEM)
HBM = pl.BlockSpec(memory_space=pl.ANY)


def dot(a, b, dims):
    return lax.dot_general(a, b, (dims, ((), ())), preferred_element_type=F32)


def local_kernel(exps_k, exps_v, q_hbm, d_hbm, kc_hbm, vc_hbm,
                 e_ref, dp_ref, kt_ref, stat_ref, q_ref, d_ref,
                 kc_ref, vc_ref, k_ref, v_ref, ke_ref, ve_ref, sems):
    sources = (exps_k, exps_v, kc_hbm, q_hbm, vc_hbm, d_hbm)
    targets = (ke_ref, ve_ref, kc_ref, q_ref, vc_ref, d_ref)
    copies = [pltpu.make_async_copy(s, t, sems.at[n]) for n, (s, t) in enumerate(zip(sources, targets))]
    for c in copies:
        c.start()
    keys = kc_ref.shape[0]
    half = keys // 2

    def dequantize(exps, codes, out):
        for g in range(2):
            wide = slice(g * HD, (g + 1) * HD)
            for b in range(keys // BLK):
                at = slice(b * BLK, (b + 1) * BLK)
                power = jnp.left_shift(1, exps[g, b] - LEAST_EXP).astype(F32) * (2.0 ** LEAST_EXP)
                out[at, wide] = (codes[at, wide].astype(F32) * power).astype(BF16)

    copies[0].wait()
    copies[2].wait()
    dequantize(ke_ref, kc_ref, k_ref)
    copies[3].wait()
    for head in range(2 * GROUP):
        g = head // GROUP
        wide = slice(g * HD, (g + 1) * HD)
        cols = slice(head * HD, (head + 1) * HD)
        q = q_ref[:, cols]
        if head == 0:
            copies[1].wait()
            copies[4].wait()
            dequantize(ve_ref, vc_ref, v_ref)
            copies[5].wait()
        d = d_ref[:, cols]
        top = None
        for c in range(2):
            at = slice(c * half, (c + 1) * half)
            s = dot(k_ref[at, wide], q, ((1,), (1,)))
            dp_ref[head, at, :] = s
            part = jnp.max(s, axis=0, keepdims=True)
            top = part if top is None else jnp.maximum(top, part)
        total = jnp.zeros((1, ROWS), F32)
        inner = jnp.zeros((1, ROWS), F32)
        for c in range(2):
            at = slice(c * half, (c + 1) * half)
            e = jnp.exp2((dp_ref[head, at, :] - top) * (SCALE * LOG2E))
            e_ref[head, at, :] = e
            total += jnp.sum(e, axis=0, keepdims=True)
            dp = dot(v_ref[at, wide], d, ((1,), (1,)))
            dp_ref[head, at, :] = dp
            inner += jnp.sum(e * dp, axis=0, keepdims=True)
        stat_ref[head:head + 1, :] = top * (SCALE * LOG2E)
        stat_ref[8 + head:9 + head, :] = total
        stat_ref[16 + head:17 + head, :] = inner
    for g in range(2):
        wide = slice(g * HD, (g + 1) * HD)
        kt_ref[wide, :] = k_ref[:, wide].T


def cache_grad_kernel(*refs):
    stats, (e_ref, dp_ref, q_ref, d_ref, ds_ref, keep_ref, send_v, send_k, both) = refs[:4], refs[4:]
    top = stats[0][0:8, :]
    for s in stats[1:]:
        top = jnp.maximum(top, s[0:8, :])
    weights = [jnp.exp2(s[0:8, :] - top) for s in stats]
    total = sum(w * s[8:16, :] for w, s in zip(weights, stats))
    inner = sum(w * s[16:24, :] for w, s in zip(weights, stats))
    delta = inner / total
    mine = weights[0] / total
    slab = both.shape[2]
    for g in range(2):
        for h in range(GROUP):
            head = g * GROUP + h
            cols = slice(head * HD, (head + 1) * HD)
            p = e_ref[head] * mine[head:head + 1, :]
            ds = (p * (dp_ref[head] - delta[head:head + 1, :])).astype(BF16)
            ds_ref[head] = ds
            kg = dot(ds, q_ref[:, cols], ((1,), (0,)))
            vg = dot(p.astype(BF16), d_ref[:, cols], ((1,), (0,)))
            key_sum = kg if h == 0 else key_sum + kg
            value_sum = vg if h == 0 else value_sum + vg
        key_low = (key_sum * SCALE).astype(BF16)
        value_low = value_sum.astype(BF16)
        for z in range(DEPTH):
            at = slice(z * slab, (z + 1) * slab)
            both[z % 2, z // 2, :, g * HD:(g + 1) * HD] = key_low[at, :]
            both[z % 2, z // 2, :, (2 + g) * HD:(3 + g) * HD] = value_low[at, :]
    side = lax.rem(lax.axis_index("section") // 2, 2)
    keep_ref[...] = both[side]
    send_k[...] = both[1 - side, :, :, :2 * HD]
    send_v[...] = both[1 - side, :, :, 2 * HD:]


def query_grad_kernel(ds_ref, kt_ref, o0, o1, o2, o3, all_ref):
    for head in range(2 * GROUP):
        g = head // GROUP
        cols = slice(head * HD, (head + 1) * HD)
        qt = dot(kt_ref[g * HD:(g + 1) * HD, :], ds_ref[head], ((1,), (0,)))
        qg = (qt.T * SCALE).astype(BF16)
        for a in range(4):
            for k in range(4):
                all_ref[k, a * 16:(a + 1) * 16, cols] = qg[(a * 4 + k) * 16:(a * 4 + k + 1) * 16, :]
    me = lax.axis_index("key")
    for by, o in enumerate((o0, o1, o2, o3)):
        o[...] = all_ref[jnp.bitwise_xor(me, by)]


def pair_kernel(keep_ref, key_ref, value_ref, out_ref):
    w = key_ref.shape[-1]
    out_ref[:, :, :w] = (keep_ref[:, :, :w].astype(F32) + key_ref[...].astype(F32)).astype(BF16)
    out_ref[:, :, w:] = (keep_ref[:, :, w:].astype(F32) + value_ref[...].astype(F32)).astype(BF16)


def project_kernel(a_ref, b_ref, c_ref, d_ref, w_ref, o0, o1, o2, o3, all_ref):
    total = sum(r[...].astype(F32) for r in (a_ref, b_ref, c_ref, d_ref)).astype(BF16)
    tile = w_ref.shape[0] // W_TILES
    for n in range(W_TILES):
        at = slice(n * tile, (n + 1) * tile)
        part = dot(total, w_ref[at, :], ((1,), (1,))).astype(BF16)
        for k in range(4):
            all_ref[k, :, at] = part[k * 16:(k + 1) * 16, :]
    me = lax.axis_index("head")
    for by, o in enumerate((o0, o1, o2, o3)):
        o[...] = all_ref[lax.rem(me + by, 4)]


def finish_kernel(kv_ref, a_ref, b_ref, c_ref, d_ref, key_ref, value_ref, input_ref):
    total = kv_ref[0].astype(F32)
    for k in range(1, kv_ref.shape[0]):
        total += kv_ref[k].astype(F32)
    width = key_ref.shape[1]
    key_ref[...] = total[:, :width]
    value_ref[...] = total[:, width:]
    input_ref[...] = sum(r[...].astype(F32) for r in (a_ref, b_ref, c_ref, d_ref)).astype(BF16)


def moved(x, axis, to):
    return lax.ppermute(x, axis, [(i, to(i)) for i in range(lax.axis_size(axis))])


def deeper(section, by):
    return (section // 2 + by) % DEPTH * 2 + section % 2


def call(kernel, outs, ins, scratch=(), limit=16, specs=None, cost=1 << 28):
    return pl.pallas_call(
        kernel,
        in_specs=specs or [VMEM] * len(ins),
        out_specs=[VMEM] * len(outs),
        out_shape=outs,
        scratch_shapes=scratch,
        compiler_params=pltpu.CompilerParams(vmem_limit_bytes=limit << 20),
        cost_estimate=pl.CostEstimate(flops=cost, bytes_accessed=1 << 20, transcendentals=0),
    )(*ins)


def step(queries, attn_grad, query_weight, key_codes, key_exps, value_codes, value_exps):
    q, d, w = queries[0], attn_grad[0], query_weight[0]
    keys, width = key_codes.shape
    heads = q.shape[1] // HD
    d_model = w.shape[0]
    on = pltpu.VMEM
    e, dp, kt, stat, q, d = call(
        local_kernel,
        [on((heads, keys, ROWS), F32), on((heads, keys, ROWS), F32), on((width, keys), BF16),
         on((24, ROWS), F32), on(q.shape, BF16), on(d.shape, BF16)],
        [pltpu.with_memory_space_constraint(x, pltpu.HBM)
         for x in (key_exps.T, value_exps.T, q, d, key_codes, value_codes)],
        scratch=[on(key_codes.shape, jnp.int32), on(key_codes.shape, jnp.int32),
                 on(key_codes.shape, BF16), on(key_codes.shape, BF16),
                 pltpu.SMEM(key_exps.shape[::-1], jnp.int32), pltpu.SMEM(key_exps.shape[::-1], jnp.int32),
                 pltpu.SemaphoreType.DMA((6,))],
        limit=16, specs=[HBM] * 6,
    )
    stats = [stat] + [moved(stat, "key", lambda i: i ^ by) for by in (1, 2, 3)]
    slab = keys // DEPTH
    half = (DEPTH // 2, slab, width)
    ds, keep, send_v, send_k = call(
        cache_grad_kernel,
        [on((heads, keys, ROWS), BF16), on((*half[:2], 2 * width), BF16), on(half, BF16), on(half, BF16)],
        (*stats, e, dp, q, d),
        scratch=[on((2, *half[:2], 2 * width), BF16)],
    )
    got_v = moved(send_v, "section", lambda i: deeper(i, 1 - 2 * (i // 2 % 2)))
    got_k = moved(send_k, "section", lambda i: deeper(i, 2 * (i // 2 % 2) - 1))
    rows = ROWS // 4
    parts = call(
        query_grad_kernel,
        [on((rows, heads * HD), BF16)] * 4, (ds, kt),
        scratch=[on((4, rows, heads * HD), BF16)],
    )
    keep, parts = lax.optimization_barrier((keep, parts))
    parts = [parts[0]] + [moved(parts[by], "key", lambda i: i ^ by) for by in (1, 2, 3)]
    (kv,) = call(pair_kernel, [jax.ShapeDtypeStruct((*half[:2], 2 * width), BF16)], (keep, got_k, got_v))
    groups = [[(2 * a + p) * 2 + xh for a in range(DEPTH // 2) for xh in range(2)] for p in range(2)]
    kv = lax.all_to_all(kv.reshape(DEPTH, slab // 2, 2 * width), "section", 0, 0, axis_index_groups=groups, tiled=True)
    parts = call(
        project_kernel, [on((rows // 4, d_model), BF16)] * 4, (*parts, w), scratch=[on((4, rows // 4, d_model), BF16)]
    )
    parts = [parts[0]] + [moved(parts[by], "head", lambda i: (i + by) % 4) for by in (1, 2, 3)]
    key_grad, value_grad, input_grad = call(
        finish_kernel,
        [jax.ShapeDtypeStruct((slab // 2, width), F32), jax.ShapeDtypeStruct((slab // 2, width), F32),
         jax.ShapeDtypeStruct((rows // 4, d_model), BF16)],
        (kv, *parts),
    )
    return input_grad[None], key_grad, value_grad


def solution(mesh):
    return jax.shard_map(
        step,
        mesh=mesh,
        in_specs=(
            P("section", None, "head"),
            P("section", None, "head"),
            P("section", None, "head"),
            P("key", "head"),
            P("key", "head"),
            P("key", "head"),
            P("key", "head"),
        ),
        out_specs=(
            P("section", ("head", "key"), None),
            P(("key", "section"), "head"),
            P(("key", "section"), "head"),
        ),
        check_vma=False,
    )
```

```python
import functools

import jax
import jax.numpy as jnp
from jax import lax
from jax.experimental import pallas as pl
from jax.experimental.pallas import tpu as pltpu
from jax.sharding import PartitionSpec as P


HQ = 24
KVH = 8
HD = 128
GROUP = HQ // KVH
ROWS = 256
BLK = 64
LOG2E = 1.4426950408889634
SCALE = HD ** -0.5
LEAST_EXP = -9
DEPTH = 8
W_TILES = 6

F32 = jnp.float32
BF16 = jnp.bfloat16

VMEM = pl.BlockSpec(memory_space=pltpu.VMEM)
HBM = pl.BlockSpec(memory_space=pl.ANY)


def dot(a, b, dims):
    return lax.dot_general(a, b, (dims, ((), ())), preferred_element_type=F32)


def local_kernel(exps_k, exps_v, q_hbm, d_hbm, kc_hbm, vc_hbm, w_hbm,
                 e_ref, dp_ref, kt_ref, stat_ref, q_ref, d_ref, w_ref,
                 kc_ref, vc_ref, k_ref, v_ref, ke_ref, ve_ref, sems):
    sources = (exps_k, exps_v, kc_hbm, q_hbm, vc_hbm, d_hbm, w_hbm)
    targets = (ke_ref, ve_ref, kc_ref, q_ref, vc_ref, d_ref, w_ref)
    copies = [pltpu.make_async_copy(s, t, sems.at[n]) for n, (s, t) in enumerate(zip(sources, targets))]
    for c in copies[:6]:
        c.start()
    keys = kc_ref.shape[0]
    half = keys // 2

    def dequantize(exps, codes, out):
        for g in range(2):
            wide = slice(g * HD, (g + 1) * HD)
            for b in range(keys // BLK):
                at = slice(b * BLK, (b + 1) * BLK)
                power = jnp.left_shift(1, exps[g, b] - LEAST_EXP).astype(F32) * (2.0 ** LEAST_EXP)
                out[at, wide] = (codes[at, wide].astype(F32) * power).astype(BF16)

    copies[0].wait()
    copies[2].wait()
    dequantize(ke_ref, kc_ref, k_ref)
    copies[3].wait()
    for head in range(2 * GROUP):
        g = head // GROUP
        wide = slice(g * HD, (g + 1) * HD)
        cols = slice(head * HD, (head + 1) * HD)
        q = q_ref[:, cols]
        if head == 0:
            copies[1].wait()
            copies[4].wait()
            dequantize(ve_ref, vc_ref, v_ref)
            copies[5].wait()
            copies[6].start()
        d = d_ref[:, cols]
        top = None
        for c in range(2):
            at = slice(c * half, (c + 1) * half)
            s = dot(k_ref[at, wide], q, ((1,), (1,)))
            dp_ref[head, at, :] = s
            part = jnp.max(s, axis=0, keepdims=True)
            top = part if top is None else jnp.maximum(top, part)
        total = jnp.zeros((1, ROWS), F32)
        inner = jnp.zeros((1, ROWS), F32)
        for c in range(2):
            at = slice(c * half, (c + 1) * half)
            e = jnp.exp2((dp_ref[head, at, :] - top) * (SCALE * LOG2E))
            e_ref[head, at, :] = e
            total += jnp.sum(e, axis=0, keepdims=True)
            dp = dot(v_ref[at, wide], d, ((1,), (1,)))
            dp_ref[head, at, :] = dp
            inner += jnp.sum(e * dp, axis=0, keepdims=True)
        stat_ref[head:head + 1, :] = top * (SCALE * LOG2E)
        stat_ref[8 + head:9 + head, :] = total
        stat_ref[16 + head:17 + head, :] = inner
    for g in range(2):
        wide = slice(g * HD, (g + 1) * HD)
        kt_ref[wide, :] = k_ref[:, wide].T
    copies[6].wait()


def cache_grad_kernel(*refs):
    stats, (e_ref, dp_ref, q_ref, d_ref, ds_ref, kv_ref, far_k, far_v) = refs[:4], refs[4:]
    top = stats[0][0:8, :]
    for s in stats[1:]:
        top = jnp.maximum(top, s[0:8, :])
    weights = [jnp.exp2(s[0:8, :] - top) for s in stats]
    total = sum(w * s[8:16, :] for w, s in zip(weights, stats))
    inner = sum(w * s[16:24, :] for w, s in zip(weights, stats))
    delta = inner / total
    mine = weights[0] / total
    slab = kv_ref.shape[1]
    for g in range(2):
        for h in range(GROUP):
            head = g * GROUP + h
            cols = slice(head * HD, (head + 1) * HD)
            p = e_ref[head] * mine[head:head + 1, :]
            ds = (p * (dp_ref[head] - delta[head:head + 1, :])).astype(BF16)
            ds_ref[head] = ds
            kg = dot(ds, q_ref[:, cols], ((1,), (0,)))
            vg = dot(p.astype(BF16), d_ref[:, cols], ((1,), (0,)))
            key_sum = kg if h == 0 else key_sum + kg
            value_sum = vg if h == 0 else value_sum + vg
        key_low = (key_sum * SCALE).astype(BF16)
        value_low = value_sum.astype(BF16)
        for z in range(DEPTH):
            at = slice(z * slab, (z + 1) * slab)
            kv_ref[z, :, g * HD:(g + 1) * HD] = key_low[at, :]
            kv_ref[z, :, (2 + g) * HD:(3 + g) * HD] = value_low[at, :]
    far = away(DEPTH // 2)
    far_k[...] = kv_ref[far, :, :2 * HD]
    far_v[...] = kv_ref[far, :, 2 * HD:]


def away(by):
    return lax.rem(lax.axis_index("section") // 2 + (by + DEPTH), DEPTH)


def added(*terms):
    return sum(t.astype(F32) for t in terms).astype(BF16)


def join_far_kernel(kv_ref, up_ref, down_ref, to_up, to_down):
    w = up_ref.shape[1]
    above, below = away(3), away(-3)
    to_up[:, :w] = kv_ref[above, :, :w]
    to_up[:, w:] = added(kv_ref[above, :, w:], up_ref[...])
    to_down[:, :w] = added(kv_ref[below, :, :w], down_ref[...])
    to_down[:, w:] = kv_ref[below, :, w:]


def join_kernel(by, kv_ref, up_ref, down_ref, to_up, to_down):
    to_up[...] = added(kv_ref[away(by)], up_ref[...])
    to_down[...] = added(kv_ref[away(-by)], down_ref[...])


def last_join_kernel(kv_ref, up_ref, down_ref, keep_ref, send_ref, both):
    rows = keep_ref.shape[0]
    mine = kv_ref[away(0)].astype(F32) + up_ref[...].astype(F32) + down_ref[...].astype(F32)
    both[0] = mine[:rows]
    both[1] = mine[rows:]
    part = lax.rem(lax.axis_index("section"), 2)
    keep_ref[...] = both[part]
    send_ref[...] = both[1 - part].astype(BF16)


def query_grad_kernel(ds_ref, kt_ref, o0, o1, o2, o3, all_ref):
    for head in range(2 * GROUP):
        g = head // GROUP
        cols = slice(head * HD, (head + 1) * HD)
        qt = dot(kt_ref[g * HD:(g + 1) * HD, :], ds_ref[head], ((1,), (0,)))
        qg = (qt.T * SCALE).astype(BF16)
        for a in range(4):
            for k in range(4):
                all_ref[k, a * 16:(a + 1) * 16, cols] = qg[(a * 4 + k) * 16:(a * 4 + k + 1) * 16, :]
    me = lax.axis_index("key")
    for by, o in enumerate((o0, o1, o2, o3)):
        o[...] = all_ref[jnp.bitwise_xor(me, by)]


def project_kernel(a_ref, b_ref, c_ref, d_ref, w_ref, o0, o1, o2, o3, all_ref):
    total = sum(r[...].astype(F32) for r in (a_ref, b_ref, c_ref, d_ref)).astype(BF16)
    tile = w_ref.shape[0] // W_TILES
    for n in range(W_TILES):
        at = slice(n * tile, (n + 1) * tile)
        part = dot(total, w_ref[at, :], ((1,), (1,))).astype(BF16)
        for k in range(4):
            all_ref[k, :, at] = part[k * 16:(k + 1) * 16, :]
    me = lax.axis_index("head")
    for by, o in enumerate((o0, o1, o2, o3)):
        o[...] = all_ref[lax.rem(me + by, 4)]


def finish_kernel(keep_ref, got_ref, a_ref, b_ref, c_ref, d_ref, key_ref, value_ref, input_ref):
    total = keep_ref[...] + got_ref[...].astype(F32)
    width = key_ref.shape[1]
    key_ref[...] = total[:, :width]
    value_ref[...] = total[:, width:]
    input_ref[...] = added(a_ref[...], b_ref[...], c_ref[...], d_ref[...])


def moved(x, axis, to):
    return lax.ppermute(x, axis, [(i, to(i)) for i in range(lax.axis_size(axis))])


def deeper(section, by):
    return (section // 2 + by) % DEPTH * 2 + section % 2


def call(kernel, outs, ins, scratch=(), limit=16, specs=None, cost=1 << 28):
    return pl.pallas_call(
        kernel,
        in_specs=specs or [VMEM] * len(ins),
        out_specs=[VMEM] * len(outs),
        out_shape=outs,
        scratch_shapes=scratch,
        compiler_params=pltpu.CompilerParams(vmem_limit_bytes=limit << 20),
        cost_estimate=pl.CostEstimate(flops=cost, bytes_accessed=1 << 20, transcendentals=0),
    )(*ins)


def step(queries, attn_grad, query_weight, key_codes, key_exps, value_codes, value_exps):
    q, d, w = queries[0], attn_grad[0], query_weight[0]
    keys, width = key_codes.shape
    heads = q.shape[1] // HD
    d_model = w.shape[0]
    on = pltpu.VMEM
    e, dp, kt, stat, q, d, w = call(
        local_kernel,
        [on((heads, keys, ROWS), F32), on((heads, keys, ROWS), F32), on((width, keys), BF16),
         on((24, ROWS), F32), on(q.shape, BF16), on(d.shape, BF16), on(w.shape, BF16)],
        [pltpu.with_memory_space_constraint(x, pltpu.HBM)
         for x in (key_exps.T, value_exps.T, q, d, key_codes, value_codes, w)],
        scratch=[on(key_codes.shape, jnp.int32), on(key_codes.shape, jnp.int32),
                 on(key_codes.shape, BF16), on(key_codes.shape, BF16),
                 pltpu.SMEM(key_exps.shape[::-1], jnp.int32), pltpu.SMEM(key_exps.shape[::-1], jnp.int32),
                 pltpu.SemaphoreType.DMA((7,))],
        limit=16, specs=[HBM] * 7,
    )
    stats = [stat] + [moved(stat, "key", lambda i: i ^ by) for by in (1, 2, 3)]
    slab = keys // DEPTH
    rows = ROWS // 4
    ds, kv, far_k, far_v = call(
        cache_grad_kernel,
        [on((heads, keys, ROWS), BF16), on((DEPTH, slab, 2 * width), BF16),
         on((slab, width), BF16), on((slab, width), BF16)],
        (*stats, e, dp, q, d),
    )
    down = moved(far_k, "section", lambda i: deeper(i, -1))
    up = moved(far_v, "section", lambda i: deeper(i, 1))
    parts = call(
        query_grad_kernel,
        [on((rows, heads * HD), BF16)] * 4, (ds, kt),
        scratch=[on((4, rows, heads * HD), BF16)],
    )
    kv, parts = lax.optimization_barrier((kv, parts))
    parts = [parts[0]] + [moved(parts[by], "key", lambda i: i ^ by) for by in (1, 2, 3)]
    whole = on((slab, 2 * width), BF16)
    up, down = call(join_far_kernel, [whole] * 2, (kv, up, down))
    down = moved(down, "section", lambda i: deeper(i, -1))
    up = moved(up, "section", lambda i: deeper(i, 1))
    up, down = call(functools.partial(join_kernel, 2), [whole] * 2, (kv, up, down))
    down = moved(down, "section", lambda i: deeper(i, -1))
    up = moved(up, "section", lambda i: deeper(i, 1))
    parts = call(
        project_kernel,
        [on((rows // 4, d_model), BF16)] * 4, (*parts, w),
        scratch=[on((4, rows // 4, d_model), BF16)],
    )
    kv, parts = lax.optimization_barrier((kv, parts))
    up, down = call(functools.partial(join_kernel, 1), [whole] * 2, (kv, up, down))
    down = moved(down, "section", lambda i: deeper(i, -1))
    up = moved(up, "section", lambda i: deeper(i, 1))
    parts = [parts[0]] + [moved(parts[by], "head", lambda i: (i + by) % 4) for by in (1, 2, 3)]
    keep, send = call(
        last_join_kernel,
        [on((slab // 2, 2 * width), F32), on((slab // 2, 2 * width), BF16)], (kv, up, down),
        scratch=[on((2, slab // 2, 2 * width), F32)],
    )
    got = moved(send, "section", lambda i: i ^ 1)
    key_grad, value_grad, input_grad = call(
        finish_kernel,
        [jax.ShapeDtypeStruct((slab // 2, width), F32), jax.ShapeDtypeStruct((slab // 2, width), F32),
         jax.ShapeDtypeStruct((rows // 4, d_model), BF16)],
        (keep, got, *parts),
    )
    return input_grad[None], key_grad, value_grad


def solution(mesh):
    return jax.shard_map(
        step,
        mesh=mesh,
        in_specs=(
            P("section", None, "head"),
            P("section", None, "head"),
            P("section", None, "head"),
            P("key", "head"),
            P("key", "head"),
            P("key", "head"),
            P("key", "head"),
        ),
        out_specs=(
            P("section", ("head", "key"), None),
            P(("key", "section"), "head"),
            P(("key", "section"), "head"),
        ),
        check_vma=False,
    )
```

```python
import jax
import jax.numpy as jnp
from jax import lax
from jax.experimental import pallas as pl
from jax.experimental.pallas import tpu as pltpu
from jax.sharding import PartitionSpec as P


HQ = 24
KVH = 8
HD = 128
GROUP = HQ // KVH
ROWS = 256
BLK = 64
LOG2E = 1.4426950408889634
SCALE = HD ** -0.5
LEAST_EXP = -9
DEPTH = 8
W_TILES = 6

F32 = jnp.float32
BF16 = jnp.bfloat16

VMEM = pl.BlockSpec(memory_space=pltpu.VMEM)
HBM = pl.BlockSpec(memory_space=pl.ANY)


def dot(a, b, dims):
    return lax.dot_general(a, b, (dims, ((), ())), preferred_element_type=F32)


def local_kernel(exps_k, exps_v, q_hbm, d_hbm, kc_hbm, vc_hbm, w_hbm,
                 e_ref, dp_ref, kt_ref, stat_ref, q_ref, d_ref, w_ref,
                 kc_ref, vc_ref, k_ref, v_ref, ke_ref, ve_ref, sems):
    sources = (exps_k, exps_v, kc_hbm, q_hbm, vc_hbm, d_hbm, w_hbm)
    targets = (ke_ref, ve_ref, kc_ref, q_ref, vc_ref, d_ref, w_ref)
    copies = [pltpu.make_async_copy(s, t, sems.at[n]) for n, (s, t) in enumerate(zip(sources, targets))]
    for c in copies[:6]:
        c.start()
    keys = kc_ref.shape[0]
    half = keys // 2

    def dequantize(exps, codes, out):
        for g in range(2):
            wide = slice(g * HD, (g + 1) * HD)
            for b in range(keys // BLK):
                at = slice(b * BLK, (b + 1) * BLK)
                power = jnp.left_shift(1, exps[g, b] - LEAST_EXP).astype(F32) * (2.0 ** LEAST_EXP)
                out[at, wide] = (codes[at, wide].astype(F32) * power).astype(BF16)

    copies[0].wait()
    copies[2].wait()
    dequantize(ke_ref, kc_ref, k_ref)
    copies[3].wait()
    for head in range(2 * GROUP):
        g = head // GROUP
        wide = slice(g * HD, (g + 1) * HD)
        cols = slice(head * HD, (head + 1) * HD)
        q = q_ref[:, cols]
        if head == 0:
            copies[1].wait()
            copies[4].wait()
            dequantize(ve_ref, vc_ref, v_ref)
            copies[5].wait()
            copies[6].start()
        d = d_ref[:, cols]
        top = None
        for c in range(2):
            at = slice(c * half, (c + 1) * half)
            s = dot(k_ref[at, wide], q, ((1,), (1,)))
            dp_ref[head, at, :] = s
            part = jnp.max(s, axis=0, keepdims=True)
            top = part if top is None else jnp.maximum(top, part)
        total = jnp.zeros((1, ROWS), F32)
        inner = jnp.zeros((1, ROWS), F32)
        for c in range(2):
            at = slice(c * half, (c + 1) * half)
            e = jnp.exp2((dp_ref[head, at, :] - top) * (SCALE * LOG2E))
            e_ref[head, at, :] = e
            total += jnp.sum(e, axis=0, keepdims=True)
            dp = dot(v_ref[at, wide], d, ((1,), (1,)))
            dp_ref[head, at, :] = dp
            inner += jnp.sum(e * dp, axis=0, keepdims=True)
        stat_ref[head:head + 1, :] = top * (SCALE * LOG2E)
        stat_ref[8 + head:9 + head, :] = total
        stat_ref[16 + head:17 + head, :] = inner
    for g in range(2):
        wide = slice(g * HD, (g + 1) * HD)
        kt_ref[wide, :] = k_ref[:, wide].T
    copies[6].wait()


def cache_grad_kernel(*refs):
    stats, (e_ref, dp_ref, q_ref, d_ref, ds_ref, kv_ref, near_down, near_up, far_k, far_v) = refs[:4], refs[4:]
    top = stats[0][0:8, :]
    for s in stats[1:]:
        top = jnp.maximum(top, s[0:8, :])
    weights = [jnp.exp2(s[0:8, :] - top) for s in stats]
    total = sum(w * s[8:16, :] for w, s in zip(weights, stats))
    inner = sum(w * s[16:24, :] for w, s in zip(weights, stats))
    delta = inner / total
    mine = weights[0] / total
    slab = kv_ref.shape[1]
    for g in range(2):
        for h in range(GROUP):
            head = g * GROUP + h
            cols = slice(head * HD, (head + 1) * HD)
            p = e_ref[head] * mine[head:head + 1, :]
            ds = (p * (dp_ref[head] - delta[head:head + 1, :])).astype(BF16)
            ds_ref[head] = ds
            kg = dot(ds, q_ref[:, cols], ((1,), (0,)))
            vg = dot(p.astype(BF16), d_ref[:, cols], ((1,), (0,)))
            key_sum = kg if h == 0 else key_sum + kg
            value_sum = vg if h == 0 else value_sum + vg
        key_low = (key_sum * SCALE).astype(BF16)
        value_low = value_sum.astype(BF16)
        for z in range(DEPTH):
            at = slice(z * slab, (z + 1) * slab)
            kv_ref[z, :, g * HD:(g + 1) * HD] = key_low[at, :]
            kv_ref[z, :, (2 + g) * HD:(3 + g) * HD] = value_low[at, :]
    for n, by in enumerate((1, 3)):
        near_down[n] = kv_ref[away(-by)]
        near_up[n] = kv_ref[away(by)]
    far = away(DEPTH // 2)
    far_k[...] = kv_ref[far, :, :2 * HD]
    far_v[...] = kv_ref[far, :, 2 * HD:]


def away(by):
    return lax.rem(lax.axis_index("section") // 2 + (by + DEPTH), DEPTH)


def total_of(*terms):
    return sum(t.astype(F32) for t in terms)


def collect_kernel(kv_ref, above_ref, below_ref, far_k, far_v,
                   down_same, down_other, up_same, up_other, keep_ref, mine_other, both):
    rows, w = keep_ref.shape[0], far_k.shape[1]
    part = lax.rem(lax.axis_index("section"), 2)
    mine = total_of(kv_ref[away(0)], above_ref[0], below_ref[0])
    for xh in range(2):
        both[xh] = mine[xh * rows:(xh + 1) * rows, :]
    keep_ref[...] = both[part]
    mine_other[...] = both[1 - part].astype(BF16)
    for by, near, far, cols, same, other in (
        (-2, above_ref, far_k, slice(0, w), down_same, down_other),
        (2, below_ref, far_v, slice(w, 2 * w), up_same, up_other),
    ):
        whole = total_of(kv_ref[away(by)], near[1])
        for xh in range(2):
            both[xh] = whole[xh * rows:(xh + 1) * rows, :]
            both[xh, :, cols] += far[xh * rows:(xh + 1) * rows, :].astype(F32)
        same[...] = both[part].astype(BF16)
        other[...] = both[1 - part].astype(BF16)


def query_grad_kernel(ds_ref, kt_ref, o0, o1, o2, o3, all_ref):
    for head in range(2 * GROUP):
        g = head // GROUP
        cols = slice(head * HD, (head + 1) * HD)
        qt = dot(kt_ref[g * HD:(g + 1) * HD, :], ds_ref[head], ((1,), (0,)))
        qg = (qt.T * SCALE).astype(BF16)
        for a in range(4):
            for k in range(4):
                all_ref[k, a * 16:(a + 1) * 16, cols] = qg[(a * 4 + k) * 16:(a * 4 + k + 1) * 16, :]
    me = lax.axis_index("key")
    for by, o in enumerate((o0, o1, o2, o3)):
        o[...] = all_ref[jnp.bitwise_xor(me, by)]


def project_kernel(a_ref, b_ref, c_ref, d_ref, w_ref, o0, o1, o2, o3, all_ref):
    total = sum(r[...].astype(F32) for r in (a_ref, b_ref, c_ref, d_ref)).astype(BF16)
    tile = w_ref.shape[0] // W_TILES
    for n in range(W_TILES):
        at = slice(n * tile, (n + 1) * tile)
        part = dot(total, w_ref[at, :], ((1,), (1,))).astype(BF16)
        for k in range(4):
            all_ref[k, :, at] = part[k * 16:(k + 1) * 16, :]
    me = lax.axis_index("head")
    for by, o in enumerate((o0, o1, o2, o3)):
        o[...] = all_ref[lax.rem(me + by, 4)]


def finish_kernel(keep_ref, *refs):
    got, parts, (key_ref, value_ref, input_ref) = refs[:5], refs[5:9], refs[9:]
    total = total_of(keep_ref[...], *(r[...] for r in got))
    width = key_ref.shape[1]
    key_ref[...] = total[:, :width]
    value_ref[...] = total[:, width:]
    input_ref[...] = total_of(*(r[...] for r in parts)).astype(BF16)


def moved(x, axis, to):
    return lax.ppermute(x, axis, [(i, to(i)) for i in range(lax.axis_size(axis))])


def deeper(by, across=0):
    return lambda section: (section // 2 + by) % DEPTH * 2 + (section % 2 ^ across)


def call(kernel, outs, ins, scratch=(), limit=16, specs=None, cost=1 << 28):
    return pl.pallas_call(
        kernel,
        in_specs=specs or [VMEM] * len(ins),
        out_specs=[VMEM] * len(outs),
        out_shape=outs,
        scratch_shapes=scratch,
        compiler_params=pltpu.CompilerParams(vmem_limit_bytes=limit << 20),
        cost_estimate=pl.CostEstimate(flops=cost, bytes_accessed=1 << 20, transcendentals=0),
    )(*ins)


def step(queries, attn_grad, query_weight, key_codes, key_exps, value_codes, value_exps):
    q, d, w = queries[0], attn_grad[0], query_weight[0]
    keys, width = key_codes.shape
    heads = q.shape[1] // HD
    d_model = w.shape[0]
    on = pltpu.VMEM
    e, dp, kt, stat, q, d, w = call(
        local_kernel,
        [on((heads, keys, ROWS), F32), on((heads, keys, ROWS), F32), on((width, keys), BF16),
         on((24, ROWS), F32), on(q.shape, BF16), on(d.shape, BF16), on(w.shape, BF16)],
        [pltpu.with_memory_space_constraint(x, pltpu.HBM)
         for x in (key_exps.T, value_exps.T, q, d, key_codes, value_codes, w)],
        scratch=[on(key_codes.shape, jnp.int32), on(key_codes.shape, jnp.int32),
                 on(key_codes.shape, BF16), on(key_codes.shape, BF16),
                 pltpu.SMEM(key_exps.shape[::-1], jnp.int32), pltpu.SMEM(key_exps.shape[::-1], jnp.int32),
                 pltpu.SemaphoreType.DMA((7,))],
        limit=16, specs=[HBM] * 7,
    )
    stats = [stat] + [moved(stat, "key", lambda i: i ^ by) for by in (1, 2, 3)]
    slab = keys // DEPTH
    rows = ROWS // 4
    near = on((2, slab, 2 * width), BF16)
    ds, kv, near_down, near_up, far_k, far_v = call(
        cache_grad_kernel,
        [on((heads, keys, ROWS), BF16), on((DEPTH, slab, 2 * width), BF16),
         near, near, on((slab, width), BF16), on((slab, width), BF16)],
        (*stats, e, dp, q, d),
    )
    above = moved(near_down, "section", deeper(-1))
    below = moved(near_up, "section", deeper(1))
    far_k = moved(far_k, "section", deeper(-2))
    far_v = moved(far_v, "section", deeper(2))
    parts = call(
        query_grad_kernel,
        [on((rows, heads * HD), BF16)] * 4, (ds, kt),
        scratch=[on((4, rows, heads * HD), BF16)],
    )
    parts = [parts[0]] + [moved(parts[by], "key", lambda i: i ^ by) for by in (1, 2, 3)]
    parts = call(
        project_kernel,
        [on((rows // 4, d_model), BF16)] * 4, (*parts, w),
        scratch=[on((4, rows // 4, d_model), BF16)],
    )
    kv, parts = lax.optimization_barrier((kv, parts))
    piece = on((slab // 2, 2 * width), BF16)
    down_same, down_other, up_same, up_other, keep, mine_other = call(
        collect_kernel,
        [piece] * 4 + [on((slab // 2, 2 * width), F32), piece],
        (kv, above, below, far_k, far_v),
        scratch=[on((2, slab // 2, 2 * width), F32)],
    )
    got = [
        moved(down_same, "section", deeper(-2)),
        moved(up_same, "section", deeper(2)),
        moved(down_other, "section", deeper(-2, 1)),
        moved(up_other, "section", deeper(2, 1)),
        moved(mine_other, "section", deeper(0, 1)),
    ]
    parts = [parts[0]] + [moved(parts[by], "head", lambda i: (i + by) % 4) for by in (1, 2, 3)]
    key_grad, value_grad, input_grad = call(
        finish_kernel,
        [jax.ShapeDtypeStruct((slab // 2, width), F32), jax.ShapeDtypeStruct((slab // 2, width), F32),
         jax.ShapeDtypeStruct((rows // 4, d_model), BF16)],
        (keep, *got, *parts),
    )
    return input_grad[None], key_grad, value_grad


def solution(mesh):
    return jax.shard_map(
        step,
        mesh=mesh,
        in_specs=(
            P("section", None, "head"),
            P("section", None, "head"),
            P("section", None, "head"),
            P("key", "head"),
            P("key", "head"),
            P("key", "head"),
            P("key", "head"),
        ),
        out_specs=(
            P("section", ("head", "key"), None),
            P(("key", "section"), "head"),
            P(("key", "section"), "head"),
        ),
        check_vma=False,
    )
```

```python
import jax
import jax.numpy as jnp
from jax import lax
from jax.experimental import pallas as pl
from jax.experimental.pallas import tpu as pltpu
from jax.sharding import PartitionSpec as P


HQ = 24
KVH = 8
HD = 128
GROUP = HQ // KVH
ROWS = 256
BLK = 64
LOG2E = 1.4426950408889634
SCALE = HD ** -0.5
LEAST_EXP = -9
DEPTH = 8
W_TILES = 6

F32 = jnp.float32
BF16 = jnp.bfloat16

VMEM = pl.BlockSpec(memory_space=pltpu.VMEM)
HBM = pl.BlockSpec(memory_space=pl.ANY)


def dot(a, b, dims):
    return lax.dot_general(a, b, (dims, ((), ())), preferred_element_type=F32)


def local_kernel(exps_k, exps_v, q_hbm, d_hbm, kc_hbm, vc_hbm, w_hbm,
                 e_ref, dp_ref, kt_ref, stat_ref, q_ref, d_ref, w_ref,
                 kc_ref, vc_ref, k_ref, v_ref, ke_ref, ve_ref, sems):
    sources = (exps_k, exps_v, kc_hbm, q_hbm, vc_hbm, d_hbm, w_hbm)
    targets = (ke_ref, ve_ref, kc_ref, q_ref, vc_ref, d_ref, w_ref)
    copies = [pltpu.make_async_copy(s, t, sems.at[n]) for n, (s, t) in enumerate(zip(sources, targets))]
    for c in copies[:6]:
        c.start()
    keys = kc_ref.shape[0]
    half = keys // 2

    def dequantize(exps, codes, out):
        for g in range(2):
            wide = slice(g * HD, (g + 1) * HD)
            for b in range(keys // BLK):
                at = slice(b * BLK, (b + 1) * BLK)
                power = jnp.left_shift(1, exps[g, b] - LEAST_EXP).astype(F32) * (2.0 ** LEAST_EXP)
                out[at, wide] = (codes[at, wide].astype(F32) * power).astype(BF16)

    copies[0].wait()
    copies[2].wait()
    dequantize(ke_ref, kc_ref, k_ref)
    copies[3].wait()
    for head in range(2 * GROUP):
        g = head // GROUP
        wide = slice(g * HD, (g + 1) * HD)
        cols = slice(head * HD, (head + 1) * HD)
        q = q_ref[:, cols]
        if head == 0:
            copies[1].wait()
            copies[4].wait()
            dequantize(ve_ref, vc_ref, v_ref)
            copies[5].wait()
            copies[6].start()
        d = d_ref[:, cols]
        top = None
        for c in range(2):
            at = slice(c * half, (c + 1) * half)
            s = dot(k_ref[at, wide], q, ((1,), (1,)))
            dp_ref[head, at, :] = s
            part = jnp.max(s, axis=0, keepdims=True)
            top = part if top is None else jnp.maximum(top, part)
        total = jnp.zeros((1, ROWS), F32)
        inner = jnp.zeros((1, ROWS), F32)
        for c in range(2):
            at = slice(c * half, (c + 1) * half)
            e = jnp.exp2((dp_ref[head, at, :] - top) * (SCALE * LOG2E))
            e_ref[head, at, :] = e
            total += jnp.sum(e, axis=0, keepdims=True)
            dp = dot(v_ref[at, wide], d, ((1,), (1,)))
            dp_ref[head, at, :] = dp
            inner += jnp.sum(e * dp, axis=0, keepdims=True)
        stat_ref[head:head + 1, :] = top * (SCALE * LOG2E)
        stat_ref[8 + head:9 + head, :] = total
        stat_ref[16 + head:17 + head, :] = inner
    for g in range(2):
        wide = slice(g * HD, (g + 1) * HD)
        kt_ref[wide, :] = k_ref[:, wide].T
    copies[6].wait()


def cache_grad_kernel(*refs):
    stats, (e_ref, dp_ref, q_ref, d_ref, ds_ref, kv_ref, near_down, near_up, far_k, far_v) = refs[:4], refs[4:]
    top = stats[0][0:8, :]
    for s in stats[1:]:
        top = jnp.maximum(top, s[0:8, :])
    weights = [jnp.exp2(s[0:8, :] - top) for s in stats]
    total = sum(w * s[8:16, :] for w, s in zip(weights, stats))
    inner = sum(w * s[16:24, :] for w, s in zip(weights, stats))
    delta = inner / total
    mine = weights[0] / total
    slab = kv_ref.shape[1]
    for g in range(2):
        for h in range(GROUP):
            head = g * GROUP + h
            cols = slice(head * HD, (head + 1) * HD)
            p = e_ref[head] * mine[head:head + 1, :]
            ds = (p * (dp_ref[head] - delta[head:head + 1, :])).astype(BF16)
            ds_ref[head] = ds
            kg = dot(ds, q_ref[:, cols], ((1,), (0,)))
            vg = dot(p.astype(BF16), d_ref[:, cols], ((1,), (0,)))
            key_sum = kg if h == 0 else key_sum + kg
            value_sum = vg if h == 0 else value_sum + vg
        key_low = (key_sum * SCALE).astype(BF16)
        value_low = value_sum.astype(BF16)
        for z in range(DEPTH):
            at = slice(z * slab, (z + 1) * slab)
            kv_ref[z, :, g * HD:(g + 1) * HD] = key_low[at, :]
            kv_ref[z, :, (2 + g) * HD:(3 + g) * HD] = value_low[at, :]
    for n, by in enumerate((1, 3)):
        near_down[n] = kv_ref[away(-by)]
        near_up[n] = kv_ref[away(by)]
    far = away(DEPTH // 2)
    far_k[...] = kv_ref[far, :, :2 * HD]
    far_v[...] = kv_ref[far, :, 2 * HD:]


def away(by):
    return lax.rem(lax.axis_index("section") // 2 + (by + DEPTH), DEPTH)


def total_of(*terms):
    return sum(t.astype(F32) for t in terms)


def collect_kernel(kv_ref, above_ref, below_ref, far_k, far_v, to_down, to_up, mine_ref):
    w = far_k.shape[1]
    down, up = kv_ref.at[away(-2)], kv_ref.at[away(2)]
    to_down[:, :w] = total_of(down[:, :w], above_ref[1, :, :w], far_k[...]).astype(BF16)
    to_down[:, w:] = total_of(down[:, w:], above_ref[1, :, w:]).astype(BF16)
    to_up[:, :w] = total_of(up[:, :w], below_ref[1, :, :w]).astype(BF16)
    to_up[:, w:] = total_of(up[:, w:], below_ref[1, :, w:], far_v[...]).astype(BF16)
    mine_ref[...] = total_of(kv_ref[away(0)], above_ref[0], below_ref[0])


def last_join_kernel(mine_ref, down_ref, up_ref, keep_ref, send_ref, both):
    rows = keep_ref.shape[0]
    mine = total_of(mine_ref[...], down_ref[...], up_ref[...])
    both[0] = mine[:rows]
    both[1] = mine[rows:]
    part = lax.rem(lax.axis_index("section"), 2)
    keep_ref[...] = both[part]
    send_ref[...] = both[1 - part].astype(BF16)


def query_grad_kernel(ds_ref, kt_ref, o0, o1, o2, o3, all_ref):
    for head in range(2 * GROUP):
        g = head // GROUP
        cols = slice(head * HD, (head + 1) * HD)
        qt = dot(kt_ref[g * HD:(g + 1) * HD, :], ds_ref[head], ((1,), (0,)))
        qg = (qt.T * SCALE).astype(BF16)
        for a in range(4):
            for k in range(4):
                all_ref[k, a * 16:(a + 1) * 16, cols] = qg[(a * 4 + k) * 16:(a * 4 + k + 1) * 16, :]
    me = lax.axis_index("key")
    for by, o in enumerate((o0, o1, o2, o3)):
        o[...] = all_ref[jnp.bitwise_xor(me, by)]


def project_kernel(a_ref, b_ref, c_ref, d_ref, w_ref, o0, o1, o2, o3, all_ref):
    total = sum(r[...].astype(F32) for r in (a_ref, b_ref, c_ref, d_ref)).astype(BF16)
    tile = w_ref.shape[0] // W_TILES
    for n in range(W_TILES):
        at = slice(n * tile, (n + 1) * tile)
        part = dot(total, w_ref[at, :], ((1,), (1,))).astype(BF16)
        for k in range(4):
            all_ref[k, :, at] = part[k * 16:(k + 1) * 16, :]
    me = lax.axis_index("head")
    for by, o in enumerate((o0, o1, o2, o3)):
        o[...] = all_ref[lax.rem(me + by, 4)]


def finish_kernel(keep_ref, *refs):
    got, parts, (key_ref, value_ref, input_ref) = refs[0], refs[1:5], refs[5:]
    total = total_of(keep_ref[...], got[...])
    width = key_ref.shape[1]
    key_ref[...] = total[:, :width]
    value_ref[...] = total[:, width:]
    input_ref[...] = total_of(*(r[...] for r in parts)).astype(BF16)


def moved(x, axis, to):
    return lax.ppermute(x, axis, [(i, to(i)) for i in range(lax.axis_size(axis))])


def deeper(by, across=0):
    return lambda section: (section // 2 + by) % DEPTH * 2 + (section % 2 ^ across)


def call(kernel, outs, ins, scratch=(), limit=16, specs=None, cost=1 << 28):
    return pl.pallas_call(
        kernel,
        in_specs=specs or [VMEM] * len(ins),
        out_specs=[VMEM] * len(outs),
        out_shape=outs,
        scratch_shapes=scratch,
        compiler_params=pltpu.CompilerParams(vmem_limit_bytes=limit << 20),
        cost_estimate=pl.CostEstimate(flops=cost, bytes_accessed=1 << 20, transcendentals=0),
    )(*ins)


def step(queries, attn_grad, query_weight, key_codes, key_exps, value_codes, value_exps):
    q, d, w = queries[0], attn_grad[0], query_weight[0]
    keys, width = key_codes.shape
    heads = q.shape[1] // HD
    d_model = w.shape[0]
    on = pltpu.VMEM
    e, dp, kt, stat, q, d, w = call(
        local_kernel,
        [on((heads, keys, ROWS), F32), on((heads, keys, ROWS), F32), on((width, keys), BF16),
         on((24, ROWS), F32), on(q.shape, BF16), on(d.shape, BF16), on(w.shape, BF16)],
        [pltpu.with_memory_space_constraint(x, pltpu.HBM)
         for x in (key_exps.T, value_exps.T, q, d, key_codes, value_codes, w)],
        scratch=[on(key_codes.shape, jnp.int32), on(key_codes.shape, jnp.int32),
                 on(key_codes.shape, BF16), on(key_codes.shape, BF16),
                 pltpu.SMEM(key_exps.shape[::-1], jnp.int32), pltpu.SMEM(key_exps.shape[::-1], jnp.int32),
                 pltpu.SemaphoreType.DMA((7,))],
        limit=16, specs=[HBM] * 7,
    )
    stats = [stat] + [moved(stat, "key", lambda i: i ^ by) for by in (1, 2, 3)]
    slab = keys // DEPTH
    rows = ROWS // 4
    near = on((2, slab, 2 * width), BF16)
    ds, kv, near_down, near_up, far_k, far_v = call(
        cache_grad_kernel,
        [on((heads, keys, ROWS), BF16), on((DEPTH, slab, 2 * width), BF16),
         near, near, on((slab, width), BF16), on((slab, width), BF16)],
        (*stats, e, dp, q, d),
    )
    above = moved(near_down, "section", deeper(-1))
    below = moved(near_up, "section", deeper(1))
    far_k = moved(far_k, "section", deeper(-2))
    far_v = moved(far_v, "section", deeper(2))
    parts = call(
        query_grad_kernel,
        [on((rows, heads * HD), BF16)] * 4, (ds, kt),
        scratch=[on((4, rows, heads * HD), BF16)],
    )
    kv, parts = lax.optimization_barrier((kv, parts))
    parts = [parts[0]] + [moved(parts[by], "key", lambda i: i ^ by) for by in (1, 2, 3)]
    whole = on((slab, 2 * width), BF16)
    down, up, mine = call(
        collect_kernel, [whole, whole, on((slab, 2 * width), F32)], (kv, above, below, far_k, far_v)
    )
    mine, parts = lax.optimization_barrier((mine, parts))
    down = moved(down, "section", deeper(-2))
    up = moved(up, "section", deeper(2))
    parts = call(
        project_kernel,
        [on((rows // 4, d_model), BF16)] * 4, (*parts, w),
        scratch=[on((4, rows // 4, d_model), BF16)],
    )
    parts = [parts[0]] + [moved(parts[by], "head", lambda i: (i + by) % 4) for by in (1, 2, 3)]
    keep, send = call(
        last_join_kernel,
        [on((slab // 2, 2 * width), F32), on((slab // 2, 2 * width), BF16)], (mine, down, up),
        scratch=[on((2, slab // 2, 2 * width), F32)],
    )
    got = moved(send, "section", deeper(0, 1))
    key_grad, value_grad, input_grad = call(
        finish_kernel,
        [jax.ShapeDtypeStruct((slab // 2, width), F32), jax.ShapeDtypeStruct((slab // 2, width), F32),
         jax.ShapeDtypeStruct((rows // 4, d_model), BF16)],
        (keep, got, *parts),
    )
    return input_grad[None], key_grad, value_grad


def solution(mesh):
    return jax.shard_map(
        step,
        mesh=mesh,
        in_specs=(
            P("section", None, "head"),
            P("section", None, "head"),
            P("section", None, "head"),
            P("key", "head"),
            P("key", "head"),
            P("key", "head"),
            P("key", "head"),
        ),
        out_specs=(
            P("section", ("head", "key"), None),
            P(("key", "section"), "head"),
            P(("key", "section"), "head"),
        ),
        check_vma=False,
    )
```

```python
import jax
import jax.numpy as jnp
from jax import lax
from jax.experimental import pallas as pl
from jax.experimental.pallas import tpu as pltpu
from jax.sharding import PartitionSpec as P


HQ = 24
KVH = 8
HD = 128
GROUP = HQ // KVH
ROWS = 256
BLK = 64
LOG2E = 1.4426950408889634
SCALE = HD ** -0.5
LEAST_EXP = -9
DEPTH = 8
W_TILES = 6

F32 = jnp.float32
BF16 = jnp.bfloat16

VMEM = pl.BlockSpec(memory_space=pltpu.VMEM)
HBM = pl.BlockSpec(memory_space=pl.ANY)


def dot(a, b, dims):
    return lax.dot_general(a, b, (dims, ((), ())), preferred_element_type=F32)


def local_kernel(exps_k, exps_v, q_hbm, d_hbm, kc_hbm, vc_hbm, w_hbm,
                 e_ref, dp_ref, kt_ref, stat_ref, q_ref, d_ref, w_ref,
                 kc_ref, vc_ref, k_ref, v_ref, ke_ref, ve_ref, sems):
    sources = (exps_k, exps_v, kc_hbm, q_hbm, vc_hbm, d_hbm, w_hbm)
    targets = (ke_ref, ve_ref, kc_ref, q_ref, vc_ref, d_ref, w_ref)
    copies = [pltpu.make_async_copy(s, t, sems.at[n]) for n, (s, t) in enumerate(zip(sources, targets))]
    for c in copies[:6]:
        c.start()
    keys = kc_ref.shape[0]
    half = keys // 2

    def dequantize(exps, codes, out):
        for g in range(2):
            wide = slice(g * HD, (g + 1) * HD)
            for b in range(keys // BLK):
                at = slice(b * BLK, (b + 1) * BLK)
                power = jnp.left_shift(1, exps[g, b] - LEAST_EXP).astype(F32) * (2.0 ** LEAST_EXP)
                out[at, wide] = (codes[at, wide].astype(F32) * power).astype(BF16)

    copies[0].wait()
    copies[2].wait()
    dequantize(ke_ref, kc_ref, k_ref)
    copies[3].wait()
    for head in range(2 * GROUP):
        g = head // GROUP
        wide = slice(g * HD, (g + 1) * HD)
        cols = slice(head * HD, (head + 1) * HD)
        q = q_ref[:, cols]
        if head == 0:
            copies[1].wait()
            copies[4].wait()
            dequantize(ve_ref, vc_ref, v_ref)
            copies[5].wait()
            copies[6].start()
        d = d_ref[:, cols]
        top = None
        for c in range(2):
            at = slice(c * half, (c + 1) * half)
            s = dot(k_ref[at, wide], q, ((1,), (1,)))
            dp_ref[head, at, :] = s
            part = jnp.max(s, axis=0, keepdims=True)
            top = part if top is None else jnp.maximum(top, part)
        total = jnp.zeros((1, ROWS), F32)
        inner = jnp.zeros((1, ROWS), F32)
        for c in range(2):
            at = slice(c * half, (c + 1) * half)
            e = jnp.exp2((dp_ref[head, at, :] - top) * (SCALE * LOG2E))
            e_ref[head, at, :] = e
            total += jnp.sum(e, axis=0, keepdims=True)
            dp = dot(v_ref[at, wide], d, ((1,), (1,)))
            dp_ref[head, at, :] = dp
            inner += jnp.sum(e * dp, axis=0, keepdims=True)
        stat_ref[head:head + 1, :] = top * (SCALE * LOG2E)
        stat_ref[8 + head:9 + head, :] = total
        stat_ref[16 + head:17 + head, :] = inner
    for g in range(2):
        wide = slice(g * HD, (g + 1) * HD)
        kt_ref[wide, :] = k_ref[:, wide].T
    copies[6].wait()


def cache_grad_kernel(*refs):
    stats, (e_ref, dp_ref, q_ref, d_ref, ds_ref, kv_ref, near_down, near_up, far_k, far_v) = refs[:4], refs[4:]
    top = stats[0][0:8, :]
    for s in stats[1:]:
        top = jnp.maximum(top, s[0:8, :])
    weights = [jnp.exp2(s[0:8, :] - top) for s in stats]
    total = sum(w * s[8:16, :] for w, s in zip(weights, stats))
    inner = sum(w * s[16:24, :] for w, s in zip(weights, stats))
    delta = inner / total
    mine = weights[0] / total
    slab = kv_ref.shape[1]
    for g in range(2):
        for h in range(GROUP):
            head = g * GROUP + h
            cols = slice(head * HD, (head + 1) * HD)
            p = e_ref[head] * mine[head:head + 1, :]
            ds = (p * (dp_ref[head] - delta[head:head + 1, :])).astype(BF16)
            ds_ref[head] = ds
            kg = dot(ds, q_ref[:, cols], ((1,), (0,)))
            vg = dot(p.astype(BF16), d_ref[:, cols], ((1,), (0,)))
            key_sum = kg if h == 0 else key_sum + kg
            value_sum = vg if h == 0 else value_sum + vg
        key_low = (key_sum * SCALE).astype(BF16)
        value_low = value_sum.astype(BF16)
        for z in range(DEPTH):
            at = slice(z * slab, (z + 1) * slab)
            kv_ref[z, :, g * HD:(g + 1) * HD] = key_low[at, :]
            kv_ref[z, :, (2 + g) * HD:(3 + g) * HD] = value_low[at, :]
    for n, by in enumerate((1, 3)):
        near_down[n] = kv_ref[away(-by)]
        near_up[n] = kv_ref[away(by)]
    far = away(DEPTH // 2)
    far_k[...] = kv_ref[far, :, :2 * HD]
    far_v[...] = kv_ref[far, :, 2 * HD:]


def away(by):
    sign = 1 - 2 * lax.rem(lax.axis_index("key"), 2)
    return lax.rem(lax.axis_index("section") // 2 + by * sign + DEPTH, DEPTH)


def total_of(*terms):
    return sum(t.astype(F32) for t in terms)


def collect_kernel(kv_ref, above_ref, below_ref, far_k, far_v, to_down, to_up, mine_ref):
    w = far_k.shape[1]
    down, up = kv_ref.at[away(-2)], kv_ref.at[away(2)]
    to_down[:, :w] = total_of(down[:, :w], above_ref[1, :, :w], far_k[...]).astype(BF16)
    to_down[:, w:] = total_of(down[:, w:], above_ref[1, :, w:]).astype(BF16)
    to_up[:, :w] = total_of(up[:, :w], below_ref[1, :, :w]).astype(BF16)
    to_up[:, w:] = total_of(up[:, w:], below_ref[1, :, w:], far_v[...]).astype(BF16)
    mine_ref[...] = total_of(kv_ref[away(0)], above_ref[0], below_ref[0])


def last_join_kernel(mine_ref, down_ref, up_ref, keep_ref, send_ref, both):
    rows = keep_ref.shape[0]
    mine = total_of(mine_ref[...], down_ref[...], up_ref[...])
    both[0] = mine[:rows]
    both[1] = mine[rows:]
    part = lax.rem(lax.axis_index("section"), 2)
    keep_ref[...] = both[part]
    send_ref[...] = both[1 - part].astype(BF16)


def query_grad_kernel(ds_ref, kt_ref, o0, o1, o2, o3, all_ref):
    for head in range(2 * GROUP):
        g = head // GROUP
        cols = slice(head * HD, (head + 1) * HD)
        qt = dot(kt_ref[g * HD:(g + 1) * HD, :], ds_ref[head], ((1,), (0,)))
        qg = (qt.T * SCALE).astype(BF16)
        for a in range(4):
            for k in range(4):
                all_ref[k, a * 16:(a + 1) * 16, cols] = qg[(a * 4 + k) * 16:(a * 4 + k + 1) * 16, :]
    me = lax.axis_index("key")
    for by, o in enumerate((o0, o1, o2, o3)):
        o[...] = all_ref[jnp.bitwise_xor(me, by)]


def project_kernel(a_ref, b_ref, c_ref, d_ref, w_ref, o0, o1, o2, o3, all_ref):
    total = sum(r[...].astype(F32) for r in (a_ref, b_ref, c_ref, d_ref)).astype(BF16)
    tile = w_ref.shape[0] // W_TILES
    for n in range(W_TILES):
        at = slice(n * tile, (n + 1) * tile)
        part = dot(total, w_ref[at, :], ((1,), (1,))).astype(BF16)
        for k in range(4):
            all_ref[k, :, at] = part[k * 16:(k + 1) * 16, :]
    me = lax.axis_index("head")
    for by, o in enumerate((o0, o1, o2, o3)):
        o[...] = all_ref[lax.rem(me + by, 4)]


def input_kernel(*refs):
    refs[4][...] = total_of(*(r[...] for r in refs[:4])).astype(BF16)


def finish_kernel(keep_ref, got_ref, key_ref, value_ref):
    width = key_ref.shape[1]
    key_ref[...] = total_of(keep_ref[:, :width], got_ref[:, :width])
    value_ref[...] = total_of(keep_ref[:, width:], got_ref[:, width:])


def moved(x, axis, to):
    return lax.ppermute(x, axis, [(i, to(i)) for i in range(lax.axis_size(axis))])


def sent(x, by):
    sections, keys = lax.axis_size("section"), lax.axis_size("key")
    pairs = []
    for i in range(sections):
        for k in range(keys):
            depth = (i // 2 + (by if k % 2 == 0 else -by)) % DEPTH
            pairs.append((i * keys + k, (depth * 2 + i % 2) * keys + k))
    return lax.ppermute(x, ("section", "key"), pairs)


def call(kernel, outs, ins, scratch=(), limit=16, specs=None, cost=1 << 28):
    return pl.pallas_call(
        kernel,
        in_specs=specs or [VMEM] * len(ins),
        out_specs=[VMEM] * len(outs),
        out_shape=outs,
        scratch_shapes=scratch,
        compiler_params=pltpu.CompilerParams(vmem_limit_bytes=limit << 20),
        cost_estimate=pl.CostEstimate(flops=cost, bytes_accessed=1 << 20, transcendentals=0),
    )(*ins)


def step(queries, attn_grad, query_weight, key_codes, key_exps, value_codes, value_exps):
    q, d, w = queries[0], attn_grad[0], query_weight[0]
    keys, width = key_codes.shape
    heads = q.shape[1] // HD
    d_model = w.shape[0]
    on = pltpu.VMEM
    e, dp, kt, stat, q, d, w = call(
        local_kernel,
        [on((heads, keys, ROWS), F32), on((heads, keys, ROWS), F32), on((width, keys), BF16),
         on((24, ROWS), F32), on(q.shape, BF16), on(d.shape, BF16), on(w.shape, BF16)],
        [pltpu.with_memory_space_constraint(x, pltpu.HBM)
         for x in (key_exps.T, value_exps.T, q, d, key_codes, value_codes, w)],
        scratch=[on(key_codes.shape, jnp.int32), on(key_codes.shape, jnp.int32),
                 on(key_codes.shape, BF16), on(key_codes.shape, BF16),
                 pltpu.SMEM(key_exps.shape[::-1], jnp.int32), pltpu.SMEM(key_exps.shape[::-1], jnp.int32),
                 pltpu.SemaphoreType.DMA((7,))],
        limit=16, specs=[HBM] * 7,
    )
    stats = [stat] + [moved(stat, "key", lambda i: i ^ by) for by in (1, 2, 3)]
    slab = keys // DEPTH
    rows = ROWS // 4
    near = on((2, slab, 2 * width), BF16)
    ds, kv, near_down, near_up, far_k, far_v = call(
        cache_grad_kernel,
        [on((heads, keys, ROWS), BF16), on((DEPTH, slab, 2 * width), BF16),
         near, near, on((slab, width), BF16), on((slab, width), BF16)],
        (*stats, e, dp, q, d),
    )
    above = sent(near_down, -1)
    below = sent(near_up, 1)
    far_k = sent(far_k, -2)
    far_v = sent(far_v, 2)
    parts = call(
        query_grad_kernel,
        [on((rows, heads * HD), BF16)] * 4, (ds, kt),
        scratch=[on((4, rows, heads * HD), BF16)],
    )
    kv, parts = lax.optimization_barrier((kv, parts))
    parts = [parts[0]] + [moved(parts[by], "key", lambda i: i ^ by) for by in (1, 2, 3)]
    parts = call(
        project_kernel,
        [on((rows // 4, d_model), BF16)] * 4, (*parts, w),
        scratch=[on((4, rows // 4, d_model), BF16)],
    )
    kv, parts = lax.optimization_barrier((kv, parts))
    whole = on((slab, 2 * width), BF16)
    down, up, mine = call(
        collect_kernel, [whole, whole, on((slab, 2 * width), F32)], (kv, above, below, far_k, far_v)
    )
    down = sent(down, -2)
    up = sent(up, 2)
    parts = [parts[0]] + [moved(parts[by], "head", lambda i: (i + by) % 4) for by in (1, 2, 3)]
    keep, send = call(
        last_join_kernel,
        [on((slab // 2, 2 * width), F32), on((slab // 2, 2 * width), BF16)], (mine, down, up),
        scratch=[on((2, slab // 2, 2 * width), F32)],
    )
    got = moved(send, "section", lambda i: i ^ 1)
    (input_grad,) = call(input_kernel, [jax.ShapeDtypeStruct((rows // 4, d_model), BF16)], parts)
    got, input_grad = lax.optimization_barrier((got, input_grad))
    key_grad, value_grad = call(
        finish_kernel,
        [jax.ShapeDtypeStruct((slab // 2, width), F32), jax.ShapeDtypeStruct((slab // 2, width), F32)],
        (keep, got),
    )
    return input_grad[None], key_grad, value_grad


def solution(mesh):
    return jax.shard_map(
        step,
        mesh=mesh,
        in_specs=(
            P("section", None, "head"),
            P("section", None, "head"),
            P("section", None, "head"),
            P("key", "head"),
            P("key", "head"),
            P("key", "head"),
            P("key", "head"),
        ),
        out_specs=(
            P("section", ("head", "key"), None),
            P(("key", "section"), "head"),
            P(("key", "section"), "head"),
        ),
        check_vma=False,
    )
```
